32 devices in a mesh: gx: 4 (over z), gy: 2 (over x), gz: 4 (over y, core).
Axes of the slice: x: 2, y: 2, z: 4, core: 2. Of those that a mesh axis runs over, the one named last changes fastest.
Arguments:
- weights: bfloat16 [32, 32, 32, 2, 8, 512], P('gx', 'gy', 'gz'), may hold values from -6 to 6
- angles: float32 [3, 32, 32, 32, 512], P(None, 'gx', 'gy', 'gz'), may hold values from -3.140625 to 3.140625
- translation: bfloat16 [8, 512, 512], replicated, may hold values from -0.09375 to 0.09375
Outputs:
- transformed: bfloat16 [32, 32, 32, 2, 8, 512], P('gx', 'gy', 'gz')
The draws below stay inside these ranges and needn't reach their ends.
All inputs are finite; a program needn't handle non-finite values.
Results may differ from the reference program's by a relative error of at most 0.025.
Values may be sent and summed in bfloat16 or wider, within the bound.
A program may use at most 128 MiB of HBM per device.

```python
import jax
import jax.numpy as jnp
from jax import lax

PX = 32
PY = 32
PZ = 32
CHEB = 512
RHS = 8
LEVELS = 3


def block_scale(key, extent, cuts, smallest, top_value):
    def one(dim, blocks):
        heights = jax.random.uniform(jax.random.fold_in(jax.random.fold_in(key, 6), dim), (blocks,), jnp.float32, smallest / len(cuts), top_value / len(cuts))
        return jnp.repeat(jnp.exp(heights), extent[dim] // blocks).reshape((-1,) + (1,) * (len(extent) - dim - 1))

    level = one(*cuts[0])
    for cut in cuts[1:]:
        level = level * one(*cut)
    return level


def scatter_about(own_key, dims, scale, most, pieces=(), dtype=jnp.bfloat16):
    loudness = block_scale(own_key, dims, pieces, -0.22, 0.18) if pieces else 1.0
    array = jax.random.normal(own_key, dims, jnp.float32) * scale * loudness
    return jnp.minimum(jnp.maximum(array, -most), most).astype(dtype)


def setup_inputs(seed: int = 0) -> dict:
    streams_of = jax.random.split(jax.random.key(seed), 4)
    weights = scatter_about(streams_of[0], (PX, PY, PZ, 2, RHS, CHEB), 1.0, 6.0, ((0, 4), (1, 2), (2, 4)))
    angles = jnp.clip(jax.random.uniform(streams_of[1], (LEVELS, PX, PY, PZ, CHEB), jnp.float32, -3.140625, 3.140625), -3.140625, 3.140625)
    translation = scatter_about(streams_of[2], (8, CHEB, CHEB), (8 * CHEB) ** -0.5, 0.09375)
    return {"weights": weights, "angles": angles, "translation": translation}


def rotate_phase(current, angle):
    real_part = current[:, :, :, 0].astype(jnp.float32)
    imag_part = current[:, :, :, 1].astype(jnp.float32)
    cosine = jnp.cos(angle)[:, :, :, None, :]
    sine = jnp.sin(angle)[:, :, :, None, :]
    rotated_re = real_part * cosine - imag_part * sine
    rotated_im = real_part * sine + imag_part * cosine
    return jnp.stack([rotated_re, rotated_im], axis=3).astype(jnp.bfloat16)


def fold_local(child_terms, dim_pos, low_span):
    dims_shape = child_terms.shape
    count = dims_shape[dim_pos]
    split = child_terms.reshape(dims_shape[:dim_pos] + (count // (2 * low_span), 2, low_span) + dims_shape[dim_pos + 1:])
    first = jnp.take(split, 0, axis=dim_pos + 1).astype(jnp.float32)
    second = jnp.take(split, 1, axis=dim_pos + 1).astype(jnp.float32)
    added = (first + second).astype(jnp.bfloat16)
    return added.reshape(dims_shape[:dim_pos] + (count // 2,) + dims_shape[dim_pos + 1:])


def insert_bit(lower, upper, dim_pos, low_span):
    dims_shape = lower.shape
    count = dims_shape[dim_pos]
    inner_shape = dims_shape[:dim_pos] + (count // low_span, low_span) + dims_shape[dim_pos + 1:]
    stacked = jnp.stack([lower.reshape(inner_shape), upper.reshape(inner_shape)], axis=dim_pos + 1)
    return stacked.reshape(dims_shape[:dim_pos] + (2 * count,) + dims_shape[dim_pos + 1:])


def translate_all(summed, translation, local_dims, chosen_bits):
    if not local_dims:
        orient = 4 * chosen_bits[0] + 2 * chosen_bits[1] + chosen_bits[2]
        matrix = lax.dynamic_index_in_dim(translation, orient, 0, keepdims=False)
        rows = summed.reshape(-1, summed.shape[-1])
        result = jnp.dot(rows, matrix, preferred_element_type=jnp.float32)
        return result.astype(jnp.bfloat16).reshape(summed.shape)
    dim_pos, low_span = local_dims[0]
    halves = []
    for t in (0, 1):
        picked = dict(chosen_bits)
        picked[dim_pos] = t
        halves.append(translate_all(summed, translation, local_dims[1:], picked))
    return insert_bit(halves[0], halves[1], dim_pos, low_span)


def reference(weights, angles, translation):
    current = weights
    size_list = (PX, PY, PZ)
    for level_idx in range(LEVELS):
        child_terms = rotate_phase(current, angles[level_idx])
        local_dims = []
        for d in range(3):
            low_span = 2 ** (size_list[d].bit_length() - 2 - level_idx)
            child_terms = fold_local(child_terms, d, low_span)
            local_dims.append((d, low_span))
        current = translate_all(child_terms, translation, local_dims, dict())
    return current
```

```python
import jax
import jax.numpy as jnp
from jax import lax
from jax.experimental import pallas as pl
from jax.experimental.pallas import tpu as pltpu
from jax.sharding import PartitionSpec as P

LEVELS = 3
AXES = ("gx", "gy", "gz")


def sincos(angle):
    half = angle * 0.5
    sq = half * half
    sin_half = -1.0 / 39916800.0
    for c in (1.0 / 362880.0, -1.0 / 5040.0, 1.0 / 120.0, -1.0 / 6.0, 1.0):
        sin_half = sin_half * sq + c
    sin_half = sin_half * half
    cos_half = 1.0 / 479001600.0
    for c in (-1.0 / 3628800.0, 1.0 / 40320.0, -1.0 / 720.0, 1.0 / 24.0, -0.5, 1.0):
        cos_half = cos_half * sq + c
    return 1.0 - 2.0 * sin_half * sin_half, 2.0 * sin_half * cos_half


def halve_sum(terms, axis_name, dim):
    count = lax.axis_size(axis_name)
    bit = lax.axis_index(axis_name) // (count // 2)
    mine = lax.dynamic_index_in_dim(terms, bit, dim, keepdims=True)
    theirs = lax.dynamic_index_in_dim(terms, 1 - bit, dim, keepdims=True)
    pairs = [(i, (i + count // 2) % count) for i in range(count)]
    got = lax.ppermute(theirs, axis_name, pairs)
    return (mine.astype(jnp.float32) + got.astype(jnp.float32)).astype(jnp.bfloat16)


def exchange_low(terms, axis_name, dim):
    count = lax.axis_size(axis_name)
    low = count // 2
    if low == 1:
        return terms
    groups = [[h * low + i for i in range(low)] for h in range(2)]
    return lax.all_to_all(
        terms, axis_name, split_axis=dim, concat_axis=dim, axis_index_groups=groups, tiled=True
    )


def rotate_sum(current, angle):
    cosine, sine = sincos(angle.astype(jnp.float32))
    cosine = cosine[..., None, :]
    sine = sine[..., None, :]
    re = current[0].astype(jnp.float32)
    im = current[1].astype(jnp.float32)
    return re * cosine - im * sine, re * sine + im * cosine


MESH = pl.DeviceIdType.MESH


def greet_all(counts):
    ids = [lax.axis_index(a) for a in AXES]
    total = counts[0] * counts[1] * counts[2]
    barrier = pltpu.get_barrier_semaphore()

    def other(r):
        rel = (r // (counts[1] * counts[2]), r // counts[2] % counts[1], r % counts[2])
        return tuple(lax.rem(i + d, c) for i, d, c in zip(ids, rel, counts))

    def greet(r, carry):
        pl.semaphore_signal(barrier, 1, device_id=other(r), device_id_type=MESH)
        return carry

    lax.fori_loop(1, total, greet, 0)
    return ids, other, lambda: pl.semaphore_wait(barrier, total - 1)


def remote(src, dst, send, recv, device):
    return pltpu.make_async_remote_copy(
        src, dst, send, recv, device_id=device, device_id_type=MESH
    )


def add(a, b):
    return (a.astype(jnp.float32) + b.astype(jnp.float32)).astype(jnp.bfloat16)


def exchange_kernel(
    counts, w_ref, a_ref, b_ref, sum_ref, ph_ref,
    w_win, a_win, cos_ref, sin_ref, term0, term1, got01, got02, got11, got12, half1, both, got3,
    p_win, p_out, w_sem, a_sem, p_sem, own_sem, send_sem, got_sem, ph_send, ph_recv,
):
    cx, cy, cz = counts
    sy, hy, _, _, _, hz = sum_ref.shape[:6]
    lz = cz
    sz = sy * hz * lz
    lanes = a_ref.shape[-1] // 128
    steps = sy * hy * hz
    (gx, gy, gz), other, arrive = greet_all(counts)
    me = (gx * cy + gy) * cz + gz

    def loads(i):
        s, h, z = i // (hy * hz), i // hz % hy, i % hz
        slot = i % 2
        out = []
        for k in range(2):
            out.append(
                pltpu.make_async_copy(
                    w_ref.at[k, :, h, :, s, pl.ds(z * lz, lz)], w_win.at[slot, k], w_sem.at[slot, k]
                )
            )
            out.append(
                pltpu.make_async_copy(a_ref.at[0, k, :, h, :, s], a_win.at[slot, k], a_sem.at[slot, k])
            )
        return out

    def phase_load(u):
        level, k = u // 2, u % 2

        def start(n, carry):
            h, lane = n // lanes, n % lanes
            for c in range(cy):
                pltpu.make_async_copy(
                    b_ref.at[1 + level, k, :, h, c, :, pl.ds(pl.multiple_of(lane * 128, 128), 128)],
                    p_win.at[u % 2, c, lane, :, pl.ds(pl.multiple_of(h * sz, sz), sz)],
                    p_sem.at[u % 2],
                ).start()
            return carry

        lax.fori_loop(0, hy * lanes, start, 0)

    def rotate(i):
        z = i % hz
        slot = i % 2
        for copy in loads(i):
            copy.wait()

        @pl.when(i + 1 < steps)
        def _():
            for copy in loads(i + 1):
                copy.start()

        def box(b, carry):
            x, c = b // cy, b % cy
            for k in range(2):
                cosine, sine = sincos(a_win[slot, k, x, c])
                cos_ref[k] = cosine
                sin_ref[k] = sine
            for k in range(2):
                for r in range(lz):
                    co = cos_ref[k, pl.ds(z * lz + r, 1), :]
                    si = sin_ref[k, pl.ds(z * lz + r, 1), :]
                    re = w_win[slot, k, x, c, r, 0].astype(jnp.float32)
                    im = w_win[slot, k, x, c, r, 1].astype(jnp.float32)
                    new_re = (re * co - im * si).astype(jnp.bfloat16)
                    new_im = (re * si + im * co).astype(jnp.bfloat16)
                    if k == 0:
                        term0[i, c, r, x, 0] = new_re
                        term0[i, c, r, x, 1] = new_im
                    else:
                        term1[i, r, c, x, 0] = new_re
                        term1[i, r, c, x, 1] = new_im
            return carry

        lax.fori_loop(0, cx * cy, box, 0)

    def along_y():
        return (gx, 1 - gy, gz)

    def along_z(r):
        return (gx, gy, lax.rem(gz + r, cz))

    def along_x(r):
        return (lax.rem(gx + r, cx), gy, gz)

    def first_send(i):
        remote(term0.at[i, 1 - gy], got01.at[i], send_sem.at[0], got_sem.at[0, i], along_y()).start()
        for r in range(1, cz):
            to = along_z(r)
            remote(
                term1.at[i, to[2]], got11.at[i, cz - r - 1], send_sem.at[1], got_sem.at[1, i], to
            ).start()

    def second_send(i):
        remote(half1.at[i, 1 - gy], got12.at[i], send_sem.at[3], got_sem.at[3, i], along_y()).start()
        for r in range(1, cz):
            to = along_z(r)
            remote(
                term0.at[i, gy, to[2]], got02.at[i, cz - r - 1], send_sem.at[2], got_sem.at[2, i], to
            ).start()

    def third_send(i):
        for r in range(1, cx):
            to = along_x(r)
            remote(
                both.at[i, to[0]], got3.at[i, cx - r - 1], send_sem.at[4], got_sem.at[4, i], to
            ).start()

    def first_sum(i):
        remote(got01.at[i], got01.at[i], send_sem.at[0], got_sem.at[0, i], along_y()).wait_recv()
        remote(got11.at[i], got11.at[i], send_sem.at[1], got_sem.at[1, i], along_z(1)).wait_recv()

        def add0(b, carry):
            term0[i, gy, b // cx, b % cx] = add(term0[i, gy, b // cx, b % cx], got01[i, b // cx, b % cx])
            return carry

        lax.fori_loop(0, lz * cx, add0, 0)

        def add1(b, carry):
            c, x = b // cx, b % cx
            for j in range(cz // 2):
                a = term1[i, gz, c, x] if j == 0 else got11[i, j - 1, c, x]
                half1[i, c, x, lax.rem(gz + j, cz // 2)] = add(a, got11[i, j + cz // 2 - 1, c, x])
            return carry

        lax.fori_loop(0, cy * cx, add1, 0)

    def second_sum(i):
        remote(got02.at[i], got02.at[i], send_sem.at[2], got_sem.at[2, i], along_z(1)).wait_recv()
        remote(got12.at[i], got12.at[i], send_sem.at[3], got_sem.at[3, i], along_y()).wait_recv()

        def add2(x, carry):
            for j in range(cz // 2):
                a = term0[i, gy, gz, x] if j == 0 else got02[i, j - 1, x]
                both[i, x, 0, lax.rem(gz + j, cz // 2)] = add(a, got02[i, j + cz // 2 - 1, x])
            for j in range(cz // 2):
                both[i, x, 1, j] = add(half1[i, gy, x, j], got12[i, x, j])
            return carry

        lax.fori_loop(0, cx, add2, 0)

    def third_sum(i):
        s, h, z = i // (hy * hz), i // hz % hy, i % hz
        remote(got3.at[i], got3.at[i], send_sem.at[4], got_sem.at[4, i], along_x(1)).wait_recv()
        for j in range(cx // 2):
            for k in range(2):
                for t in range(cz // 2):
                    a = both[i, gx, k, t] if j == 0 else got3[i, j - 1, k, t]
                    sum_ref[s, h, lax.rem(gx + j, cx // 2), k, t, z] = add(
                        a, got3[i, j + cx // 2 - 1, k, t]
                    )

    def phases(u):
        level, k = u // 2, u % 2
        pltpu.make_async_copy(p_win.at[u % 2], p_win.at[u % 2], p_sem.at[u % 2]).wait()

        rows = hy * sy * hz

        def gather(b, carry):
            c, x = b // cx, b % cx
            for z in range(cz):
                for lane in range(lanes):
                    p_out[
                        level, (x * cy + c) * cz + z, k, :, lane * 128 : (lane + 1) * 128
                    ] = p_win[u % 2, c, lane, x, pl.ds(z, rows, stride=lz), :].astype(jnp.bfloat16)
            return carry

        lax.fori_loop(0, cx * cy, gather, 0)

        @pl.when(u < 2)
        def _():
            phase_load(u + 2)

        @pl.when(k == 1)
        def _():
            pltpu.make_async_copy(p_out.at[level, me], ph_ref.at[level, me], own_sem.at[level]).start()

            def send(r, carry):
                to = other(r)
                at = (to[0] * cy + to[1]) * cz + to[2]
                remote(
                    p_out.at[level, at], ph_ref.at[level, me], ph_send.at[level], ph_recv.at[level], to
                ).start()
                return carry

            lax.fori_loop(1, cx * cy * cz, send, 0)

    for copy in loads(0):
        copy.start()
    for u in range(2):
        phase_load(u)
    rotate(0)
    arrive()

    def step(i, carry):
        @pl.when(i < steps)
        def _():
            first_send(i)

        @pl.when(i < 4)
        def _():
            phases(i)

        @pl.when(i + 1 < steps)
        def _():
            rotate(i + 1)

        @pl.when(jnp.logical_and(i >= 1, i < steps + 1))
        def _():
            first_sum(i - 1)
            second_send(i - 1)

        @pl.when(jnp.logical_and(i >= 2, i < steps + 2))
        def _():
            second_sum(i - 2)
            third_send(i - 2)

        @pl.when(i >= 3)
        def _():
            third_sum(i - 3)

        return carry

    lax.fori_loop(0, steps + 3, step, 0)
    for level in range(2):
        rest = pl.ds(0, cx * cy * cz - 1)
        pltpu.make_async_copy(p_out.at[level, me], ph_ref.at[level, me], own_sem.at[level]).wait()
        remote(
            p_out.at[level, rest], ph_ref.at[level, rest], ph_send.at[level], ph_recv.at[level], other(1)
        ).wait()
    for n, ref in enumerate((got01, got11, got02, got12, got3)):
        remote(ref, ref, send_sem.at[n], got_sem.at[n, 0], other(1)).wait_send()


def exchange(weights, angles, counts, low):
    cx, cy, cz = counts
    X, Y, Z, _, R, K = weights.shape
    hx, hy, hz, sy = X // low[0], Y // low[1], Z // low[2], low[1] // cy
    steps = sy * hy * hz
    total = cx * cy * cz
    rows = hy * sy * hz
    bf = jnp.bfloat16
    unit = (2, R, K)

    def vm(*shape):
        return pltpu.VMEM(shape + unit, bf)

    dma = pltpu.SemaphoreType.DMA
    return pl.pallas_call(
        lambda *refs: exchange_kernel(counts, *refs),
        in_specs=[pl.BlockSpec(memory_space=pl.ANY)] * 3,
        out_specs=[pl.BlockSpec(memory_space=pltpu.VMEM), pl.BlockSpec(memory_space=pl.ANY)],
        out_shape=[
            jax.ShapeDtypeStruct((sy, hy, cx // 2, hx, cz // 2, hz) + unit, bf),
            jax.ShapeDtypeStruct((LEVELS - 1, total, hx, rows, K), bf),
        ],
        scratch_shapes=[
            vm(2, 2, cx, cy, cz),
            pltpu.VMEM((2, 2, cx, cy, Z, K), jnp.float32),
            pltpu.VMEM((2, Z, K), jnp.float32),
            pltpu.VMEM((2, Z, K), jnp.float32),
            vm(steps, cy, cz, cx),
            vm(steps, cz, cy, cx),
            vm(steps, cz, cx),
            vm(steps, cz - 1, cx),
            vm(steps, cz - 1, cy, cx),
            vm(steps, cx, cz // 2),
            vm(steps, cy, cx, cz // 2),
            vm(steps, cx, 2, cz // 2),
            vm(steps, cx - 1, 2, cz // 2),
            pltpu.VMEM((2, cy, K // 128, cx, hy * sy * Z, 128), jnp.float32),
            pltpu.VMEM((LEVELS - 1, total, hx, rows, K), bf),
            dma((2, 2)),
            dma((2, 2)),
            dma((2,)),
            dma((LEVELS - 1,)),
            dma((5,)),
            dma((5, steps)),
            dma((LEVELS - 1,)),
            dma((LEVELS - 1,)),
        ],
        compiler_params=pltpu.CompilerParams(
            collective_id=0, has_side_effects=True, vmem_limit_bytes=62 * 2**20
        ),
        name="exchange",
    )(
        weights.reshape(hx, cx, hy, cy, sy, Z, 2, R, K),
        angles.reshape(LEVELS, hx, cx, hy, cy, sy, Z, K),
        angles.reshape(LEVELS, hx, cx, hy, cy, sy * Z, K),
    )


def middle_kernel(
    counts, s_ref, p_ref, t_ref, o_ref, cos_ref, sin_ref, buf0, buf1, mid_ref, st_ref,
    own_sem, send_sem, got_sem,
):
    cx, cy, cz = counts
    sy = s_ref.shape[0]
    unit = s_ref.shape[3]
    R = o_ref.shape[4]
    total = cx * cy * cz
    (gx, gy, gz), other, arrive = greet_all(counts)
    me = (gx * cy + gy) * cz + gz
    bufs = (buf0, buf1)

    def turn(buf, base, level, q, row):
        re = buf[base : base + R, :]
        im = buf[base + R : base + 2 * R, :]
        co = cos_ref[level, q, row : row + 1, :]
        si = sin_ref[level, q, row : row + 1, :]
        return re * co - im * si, re * si + im * co

    def total_of(buf, terms):
        acc = None
        for term in terms:
            new = turn(buf, *term)
            acc = new if acc is None else (acc[0] + new[0], acc[1] + new[1])
        return acc

    def target(j):
        dx, dy, dz = 1 - j // 4, 1 - j // 2 % 2, 1 - j % 2
        return (
            lax.rem(gx // 2 + dx, 2),
            lax.rem(gy + dy, 2),
            lax.rem(gz // 2 + dz, 2),
        )

    def owner(j, q):
        tx, ty, tz = target(j)
        return (tx * 2 + q // 2, ty, tz * 2 + q % 2)

    def step(j, carry):
        tx, ty, tz = target(j)
        t4 = 4 * tx + 2 * ty + tz
        for q in range(4):
            to = owner(j, q)
            at = (to[0] * cy + to[1]) * cz + to[2]
            for level in range(LEVELS - 1):
                for x in range(2):
                    cosine, sine = sincos(p_ref[level, at, x].astype(jnp.float32))
                    cos_ref[level, q * 2 + x] = cosine
                    sin_ref[level, q * 2 + x] = sine

        def first_dot(p):
            s, y2 = p // 2, p % 2
            for y3 in range(2):
                bufs[p % 2][y3 * unit : (y3 + 1) * unit, :] = jnp.dot(
                    s_ref[s, y3, y2], t_ref[t4], preferred_element_type=jnp.float32
                )

        def first_turn(p):
            s, y2 = p // 2, p % 2
            for x2 in range(2):
                for z2 in range(2):
                    terms = []
                    for y3 in range(2):
                        for x3 in range(2):
                            for z3 in range(2):
                                box = ((x3 * 2 + x2) * 2 + z3) * 2 + z2
                                row = ((y3 * 2 + y2) * sy + s) * 2 + z2
                                terms.append(
                                    (y3 * unit + box * 2 * R, 0, (x3 * 2 + z3) * 2 + x2, row)
                                )
                    re, im = total_of(bufs[p % 2], terms)
                    at = (((s * 2 + y2) * 2 + x2) * 2 + z2) * 2 * R
                    mid_ref[at : at + R, :] = re.astype(jnp.bfloat16)
                    mid_ref[at + R : at + 2 * R, :] = im.astype(jnp.bfloat16)

        def second_dot(t):
            bufs[t % 2][0 : mid_ref.shape[0], :] = jnp.dot(
                mid_ref[...], t_ref[t], preferred_element_type=jnp.float32
            )

        def second_turn(t):
            t3x, t3y, t3z = t // 4, t // 2 % 2, t % 2
            q = t3x * 2 + t3z
            for s in range(sy):
                terms = []
                for y2 in range(2):
                    for x2 in range(2):
                        for z2 in range(2):
                            at = (((s * 2 + y2) * 2 + x2) * 2 + z2) * 2 * R
                            row = ((t3y * 2 + y2) * sy + s) * 2 + z2
                            terms.append((at, 1, q * 2 + x2, row))
                re, im = total_of(bufs[t % 2], terms)
                st_ref[j, q, t3y, s, 0] = re.astype(jnp.bfloat16)
                st_ref[j, q, t3y, s, 1] = im.astype(jnp.bfloat16)

        first_dot(0)
        for p in range(2 * sy):
            if p + 1 < 2 * sy:
                first_dot(p + 1)
            first_turn(p)
        second_dot(0)
        for t in range(8):
            if t + 1 < 8:
                second_dot(t + 1)
            second_turn(t)

        @pl.when(j == 0)
        def _():
            arrive()

        for q in range(4):
            to = owner(j, q)
            at = (to[0] * cy + to[1]) * cz + to[2]

            @pl.when(at == me)
            def _():
                pltpu.make_async_copy(st_ref.at[j, q], o_ref.at[me], own_sem).start()

            @pl.when(at != me)
            def _():
                remote(st_ref.at[j, q], o_ref.at[me], send_sem, got_sem, to).start()

        return carry

    lax.fori_loop(0, 8, step, 0)
    rest = o_ref.at[pl.ds(0, total - 1)]
    pltpu.make_async_copy(o_ref.at[me], o_ref.at[me], own_sem).wait()
    remote(rest, rest, send_sem, got_sem, other(1)).wait()


def middle(summed, ph, translation, counts):
    cx, cy, cz = counts
    sy, hy, x3, hx, z3, hz, _, R, K = summed.shape
    unit = x3 * hx * z3 * hz * 2 * R
    total = cx * cy * cz
    rows = hy * sy * hz
    f32, bf = jnp.float32, jnp.bfloat16
    dma = pltpu.SemaphoreType.DMA
    return pl.pallas_call(
        lambda *refs: middle_kernel(counts, *refs),
        in_specs=[pl.BlockSpec(memory_space=pltpu.VMEM)] * 3,
        out_specs=pl.BlockSpec(memory_space=pl.ANY),
        out_shape=jax.ShapeDtypeStruct((total, 2, sy, 2, R, K), bf),
        scratch_shapes=[
            pltpu.VMEM((LEVELS - 1, 8, rows, K), f32),
            pltpu.VMEM((LEVELS - 1, 8, rows, K), f32),
            pltpu.VMEM((2 * unit, K), f32),
            pltpu.VMEM((2 * unit, K), f32),
            pltpu.VMEM((sy * 8 * 2 * R, K), bf),
            pltpu.VMEM((8, 4, 2, sy, 2, R, K), bf),
            dma,
            dma,
            dma,
        ],
        compiler_params=pltpu.CompilerParams(
            collective_id=1, has_side_effects=True, vmem_limit_bytes=48 * 2**20
        ),
        name="middle",
    )(summed.reshape(sy, 2, hy // 2, unit, K), ph, translation)


def fast_shards(weights, angles, translation, counts, low):
    cx, cy, cz = counts
    summed, ph = exchange(weights, angles, counts, low)
    final = middle(summed, ph, translation, counts)
    sy, R, K = summed.shape[0], weights.shape[4], weights.shape[5]
    back = final.reshape(cx, cy, cz, 2, sy, 2, R, K).transpose(3, 5, 0, 1, 4, 2, 6, 7)
    back = back.reshape(1, 2, 1, 2, low[0], low[1], low[2], R, K)
    return last_translate(back, translation.reshape(2, 2, 2, K, K), weights.shape)


def shards(weights, angles, translation):
    counts = [lax.axis_size(a) for a in AXES]
    count_x, count_y, count_z = counts
    devices = count_x * count_y * count_z
    count_yz = count_y * count_z
    top = 2**LEVELS
    hx, hy, hz = (top // c for c in counts)
    lx, ly, lz = (weights.shape[0] // hx, weights.shape[1] // hy, weights.shape[2] // hz)
    rhs, cheb = weights.shape[4], weights.shape[5]
    blocks = lx * ly * lz
    share = blocks * rhs // devices
    block_share = max(1, blocks // devices)
    rhs_share = share // block_share
    repeat = max(1, devices // blocks)
    C = hx * hy * hz
    if (hx, hy, hz) == (2, 4, 2) and (lx, ly, lz) == (count_x, 2 * count_y, count_z):
        return fast_shards(weights, angles, translation, counts, (lx, ly, lz))

    ph = angles[1:].astype(jnp.bfloat16)
    ph = ph.reshape(LEVELS - 1, hx, lx, hy, ly, hz, lz, cheb).transpose(1, 3, 5, 0, 2, 4, 6, 7)
    ph = ph.reshape(1, 1, hx, hy, hz, LEVELS - 1, blocks, 1, cheb)
    ph = jnp.broadcast_to(ph, ph.shape[:7] + (repeat, cheb))
    ph = ph.reshape(
        1, 1, hx, hy, hz, LEVELS - 1, count_x, blocks * repeat // count_x, cheb
    )
    ph = lax.all_to_all(ph, "gx", split_axis=6, concat_axis=0, tiled=True)
    ph = lax.all_to_all(ph, ("gy", "gz"), split_axis=7, concat_axis=1, tiled=True)
    ph = ph.reshape(count_x, count_y, count_z, hx, hy, hz, LEVELS - 1, block_share, cheb)
    ph = ph.transpose(6, 0, 3, 1, 4, 2, 5, 7, 8)
    ph = ph.reshape(LEVELS - 1, top, top, top, block_share, cheb)

    parts = [
        v.reshape(C, 2, count_x // 2, 2, count_y // 2, 2, count_z // 2, share, cheb)
        for v in first_rotate(weights, angles[0], (lx, ly, lz))
    ]
    where = {"gx": 1, "gy": 3, "gz": 5}
    orders = [("gx", "gy", "gz"), ("gy", "gz", "gx"), ("gz", "gx", "gy")]
    cuts = [C * i // 3 for i in range(4)]
    streams = {}
    for p in range(2):
        for k in range(3):
            if cuts[k + 1] > cuts[k]:
                streams[p, k] = parts[p][cuts[k] : cuts[k + 1]]
    for step in range(3):
        for p, k in list(streams):
            name = orders[k][step]
            streams[p, k] = halve_sum(streams[p, k], name, where[name])
    both = jnp.stack(
        [jnp.concatenate([streams[p, k] for k in range(3) if (p, k) in streams]) for p in range(2)]
    )
    both = both.reshape(2, C, count_x // 2, count_y // 2, count_z // 2, share, cheb)
    for dim, name in ((2, "gx"), (3, "gy"), (4, "gz")):
        both = exchange_low(both, name, dim)
    both = both.reshape(
        2, hx, hy, hz, count_x // 2, count_y // 2, count_z // 2, block_share, rhs_share, cheb
    )
    summed = both.transpose(0, 4, 1, 5, 2, 6, 3, 7, 8, 9)
    q = top // 2
    summed = summed.reshape(2, q * q * q * share, cheb)

    def translate(s):
        return jnp.einsum(
            "crk,tkn->ctrn", s, translation, preferred_element_type=jnp.float32
        ).astype(jnp.bfloat16)

    tail = (block_share, rhs_share, cheb)
    w = translate(summed)
    w = w.reshape((2, 2, 2, 2, 2, 2, 2, 2, 2, 2) + tail)
    ang = ph[0].reshape((2,) * 9 + (block_share, cheb))
    ang = ang.transpose(0, 3, 6, 1, 2, 4, 5, 7, 8, 9, 10)
    r, i = rotate_sum(w, ang)
    summed = jnp.stack([r.sum((3, 5, 7)), i.sum((3, 5, 7))]).astype(jnp.bfloat16)
    w = translate(summed.reshape(2, q * q * q * share, cheb))
    w = w.reshape((2,) + (2,) * 9 + tail)
    ang = ph[1].reshape((2,) * 9 + (block_share, cheb))
    ang = ang.transpose(1, 4, 7, 0, 3, 6, 2, 5, 8, 9, 10)
    r, i = rotate_sum(w, ang)
    summed = jnp.stack([r.sum((6, 7, 8)), i.sum((6, 7, 8))]).astype(jnp.bfloat16)
    summed = summed.transpose(4, 1, 5, 2, 6, 3, 0, 7, 8, 9)
    summed = summed.reshape(q, q, q, 2, share, cheb)
    keep = []
    for d, c in enumerate(counts):
        if c > q:
            summed = jnp.repeat(summed, c // q, axis=d)
        keep.append(max(1, q // c))
    kx, ky, kz = keep
    leaving = summed.reshape(count_x, kx, count_y, ky, count_z, kz, 2, share, cheb)
    leaving = leaving.transpose(0, 2, 4, 1, 3, 5, 6, 7, 8)
    leaving = leaving.reshape(count_x, count_yz, kx, ky, kz, 2, 1, share, cheb)
    back = lax.all_to_all(leaving, "gx", split_axis=0, concat_axis=6, tiled=True)
    back = lax.all_to_all(back, ("gy", "gz"), split_axis=1, concat_axis=7, tiled=True)
    back = back.reshape(kx, ky, kz, 2, lx, ly, lz, rhs, cheb)

    mats = translation.reshape(2, 2, 2, cheb, cheb)
    for d, (c, name) in enumerate(zip(counts, AXES)):
        if c > q:
            mats = lax.dynamic_index_in_dim(mats, lax.axis_index(name) % 2, d, keepdims=True)
    return last_translate(back, mats, weights.shape)


def last_kernel(e_ref, t_ref, o_ref):
    rows = e_ref[0, 0]
    lx, ly, kz, nz, m, cheb = (o_ref.shape[1],) + tuple(o_ref.shape[3:])
    for z in range(nz):
        r = jnp.dot(rows, t_ref[0, 0, z], preferred_element_type=jnp.float32)
        o_ref[0, :, 0, :, :, z] = r.astype(jnp.bfloat16).reshape(lx, ly, kz, m, cheb)


def last_translate(back, mats, out_shape):
    kx, ky, kz, _, lx, ly, lz, rhs, cheb = back.shape
    nx, ny, nz = mats.shape[:3]
    m = lz * 2 * rhs
    rows = back.transpose(0, 1, 4, 5, 2, 6, 3, 7, 8).reshape(kx, ky, lx * ly * kz * m, cheb)
    out = pl.pallas_call(
        last_kernel,
        grid=(nx, ny, kx, ky),
        in_specs=[
            pl.BlockSpec((1, 1, lx * ly * kz * m, cheb), lambda x, y, a, b: (a, b, 0, 0)),
            pl.BlockSpec((1, 1, nz, cheb, cheb), lambda x, y, a, b: (x, y, 0, 0, 0)),
        ],
        out_specs=pl.BlockSpec(
            (1, lx, 1, ly, kz, nz, m, cheb),
            lambda x, y, a, b: (a * nx + x, 0, b * ny + y, 0, 0, 0, 0, 0),
        ),
        out_shape=jax.ShapeDtypeStruct(
            (kx * nx, lx, ky * ny, ly, kz, nz, m, cheb), jnp.bfloat16
        ),
        compiler_params=pltpu.CompilerParams(vmem_limit_bytes=40 * 2**20),
        name="last_translate",
    )(rows, mats)
    return out.reshape(out_shape)


def first_kernel(w_ref, a_ref, re_ref, im_ref, cos_ref, sin_ref):
    ly, count_z = a_ref.shape[3], a_ref.shape[4]
    lz = re_ref.shape[5]
    cosine, sine = sincos(a_ref[0, 0, 0])
    cos_ref[...] = cosine
    sin_ref[...] = sine

    @pl.loop(0, ly)
    def _(l):
        for z in range(count_z):
            c = cos_ref[l, z : z + 1, :]
            s = sin_ref[l, z : z + 1, :]
            re = w_ref[0, 0, 0, l, z, 0].astype(jnp.float32)
            im = w_ref[0, 0, 0, l, z, 1].astype(jnp.float32)
            re_ref[0, 0, z // lz, 0, l, z % lz] = (re * c - im * s).astype(jnp.bfloat16)
            im_ref[0, 0, z // lz, 0, l, z % lz] = (re * s + im * c).astype(jnp.bfloat16)


def first_rotate(weights, angle, low):
    lx, ly, lz = low
    sx, sy, sz, _, rhs, cheb = weights.shape
    hx, hy, hz = sx // lx, sy // ly, sz // lz
    shape = (hx, hy, hz, lx, ly, lz, rhs, cheb)
    out = jax.ShapeDtypeStruct(shape, jnp.bfloat16)
    spec = pl.BlockSpec(
        (1, 1, hz, 1, ly, lz, rhs, cheb), lambda a, x, b: (a, b, 0, x, 0, 0, 0, 0)
    )
    return pl.pallas_call(
        first_kernel,
        grid=(hx, lx, hy),
        in_specs=[
            pl.BlockSpec(
                (1, 1, 1, ly, sz, 2, rhs, cheb), lambda a, x, b: (a, x, b, 0, 0, 0, 0, 0)
            ),
            pl.BlockSpec((1, 1, 1, ly, sz, cheb), lambda a, x, b: (a, x, b, 0, 0, 0)),
        ],
        out_specs=[spec, spec],
        out_shape=[out, out],
        scratch_shapes=[pltpu.VMEM((ly, sz, cheb), jnp.float32)] * 2,
        compiler_params=pltpu.CompilerParams(vmem_limit_bytes=40 * 2**20),
        name="first_rotate",
    )(
        weights.reshape(hx, lx, hy, ly, sz, 2, rhs, cheb),
        angle.reshape(hx, lx, hy, ly, sz, cheb),
    )


def solution(mesh):
    in_specs = (P("gx", "gy", "gz", None, None, None), P(None, "gx", "gy", "gz", None), P())
    out_specs = P("gx", "gy", "gz", None, None, None)
    return jax.shard_map(shards, mesh=mesh, in_specs=in_specs, out_specs=out_specs, check_vma=False)
```
